512 devices in a mesh: user: 512 (over z, x, y, core).
Axes of the slice: x: 4, y: 4, z: 16, core: 2. Of those that a mesh axis runs over, the one named last changes fastest.
Arguments:
- ratings: bfloat16 [512, 3, 6, 128, 128], P('user'), may hold values from -6 to 6
- tile_index: int32 [512, 3, 6], P('user'), may hold values from 0 to 8, as said below
- tile_count: int32 [512, 3], P('user'), may hold values from 1 to 6, as said below
- side_features: bfloat16 [196608, 1024], P('user'), may hold values from -6 to 6
- user_factors: float32 [196608, 256], P('user'), may hold values from -3 to 3
- item_factors: float32 [196608, 256], P('user'), may hold values from -3 to 3
- prior_weights: float32 [1024, 256], replicated, may hold values from -0.1875 to 0.1875
- user_noise: bfloat16 [3, 196608, 256], P(None, 'user'), may hold values from -6 to 6
- item_noise: bfloat16 [3, 196608, 256], P(None, 'user'), may hold values from -6 to 6
Outputs:
- users_out: float32 [196608, 256], P('user')
- items_held: float32 [196608, 256], P('user')
- weights_out: float32 [1024, 256], P('user')
The draws below stay inside these ranges and needn't reach their ends.
Inputs may be any that keep to these rules, and one draw needn't show every extreme that they name: `tile_index`: code r * 3 + c of a tile; the codes of one device and stratum are distinct. `tile_count`: live slots are the first ones; in every stratum some device has 6.
All inputs are finite; a program needn't handle non-finite values.
Results may differ from the reference program's by a relative error of at most 0.0013.
The reference program's roundings to bfloat16 on the way (of `offset` and `errb`) count: a program that leaves them out, or rounds other values in their place, can miss the bound.
Values sent between devices are 32-bit elements; how exact they have to be, the bound alone decides.
A program may use at most 64 MiB of HBM per device.

```python
import math
import jax
import jax.numpy as jnp
from jax import lax

RANK = 256
FEAT = 1024
TILE = 128
STRATA = 3
USR_DEV = 384
MAXT = 6
USERS = 196608
ITEMS = 196608
N_USER = 512


def draw_tile_index(key, part):
    grid = USR_DEV // TILE
    cells = grid * grid
    scores = jax.random.randint(key, (N_USER, STRATA, cells), 0, 1 << 18) * 4096 + jnp.arange(cells, dtype=jnp.int32)
    order = jnp.argsort(scores, axis=-1, stable=True)
    return order[:, :, :MAXT].astype(jnp.int32)


def draw_tile_count(key, part):
    first, second = jax.random.split(jax.random.fold_in(key, 7))
    counts = jax.random.randint(first, (N_USER, STRATA), 1, MAXT + 1)
    heavy = jax.random.randint(second, (STRATA,), 0, N_USER)
    place = jnp.arange(N_USER, dtype=jnp.int32)[:, None] == heavy[None, :]
    return jnp.where(place, MAXT, counts).astype(jnp.int32)


def draw_side_features(key, part):
    inner = jax.random.fold_in(key, 11)
    values = jnp.clip(jax.random.normal(inner, (USERS, FEAT), jnp.float32), -6.0, 6.0)
    return values.astype(jnp.bfloat16)


def block_levels(stream_key, dims, cuts, least, largest):
    def one(dim, shards_of):
        draws = jax.random.uniform(jax.random.fold_in(jax.random.fold_in(stream_key, 6), dim), (shards_of,), jnp.float32, least / len(cuts), largest / len(cuts))
        return jnp.repeat(jnp.exp(draws), dims[dim] // shards_of).reshape((-1,) + (1,) * (len(dims) - dim - 1))

    level = one(*cuts[0])
    for cut in cuts[1:]:
        level = level * one(*cut)
    return level


def gaussian(own_key, dims, scale, reach, pieces=(), held_as=jnp.bfloat16):
    array = scale * jax.random.normal(own_key, dims, jnp.float32)
    if pieces:
        array = array * block_levels(own_key, dims, pieces, -0.22, 0.18)
    return jnp.clip(array, -reach, reach).astype(held_as)


def setup_inputs(seed: int = 0) -> dict:
    seeds = jax.random.split(jax.random.key(seed), 10)
    return {
        "ratings": gaussian(seeds[0], (N_USER, STRATA, MAXT, TILE, TILE), 1.0, 6.0, ((0, 512),)),
        "tile_index": draw_tile_index(jax.random.fold_in(seeds[9], 71), 0),
        "tile_count": draw_tile_count(jax.random.fold_in(seeds[9], 71), 0),
        "side_features": draw_side_features(jax.random.fold_in(seeds[9], 71), 0),
        "user_factors": gaussian(seeds[4], (USERS, RANK), 0.5, 3.0, ((0, 512),), jnp.float32),
        "item_factors": gaussian(seeds[5], (ITEMS, RANK), 0.5, 3.0, ((0, 512),), jnp.float32),
        "prior_weights": gaussian(seeds[6], (FEAT, RANK), FEAT ** -0.5, 0.1875, (), jnp.float32),
        "user_noise": gaussian(seeds[7], (STRATA, USERS, RANK), 1.0, 6.0, ((1, 512),)),
        "item_noise": gaussian(seeds[8], (STRATA, ITEMS, RANK), 1.0, 6.0, ((1, 512),)),
    }


step_size = 0.01
prior_prec = 8.0
item_prec = 1.0
weight_decay = 1.0
rate_scale = 0.04

def reference(ratings, tile_index, tile_count, side_features, user_factors, item_factors, prior_weights, user_noise, item_noise):
    grid = USR_DEV // TILE
    rate = rate_scale / (USR_DEV * N_USER)
    noise_scale = math.sqrt(2.0 * step_size)
    users = user_factors
    items = item_factors
    weights = prior_weights
    slot = jnp.arange(MAXT, dtype=jnp.int32)
    for stratum in range(STRATA):
        mean = jnp.dot(side_features, weights.astype(jnp.bfloat16), preferred_element_type=jnp.float32)
        offset = (users - mean).astype(jnp.bfloat16)
        user_b = lax.optimization_barrier(users.astype(jnp.bfloat16)).reshape(N_USER, grid, TILE, RANK)
        item_b = lax.optimization_barrier(items.astype(jnp.bfloat16)).reshape(N_USER, grid, TILE, RANK)
        codes = tile_index[:, stratum]
        live = (slot[None, :] < tile_count[:, stratum][:, None]).astype(jnp.float32)

        def one(inputs):
            tiles, code, mask, ub, vb = inputs
            rows = code // grid
            cols = code % grid
            urows = ub[rows].astype(jnp.float32)
            vrows = vb[cols].astype(jnp.float32)
            err = tiles.astype(jnp.float32) - jnp.einsum('tak,tbk->tab', urows, vrows)
            err = err * mask[:, None, None]
            sse = jnp.sum(err * err)
            errb = lax.optimization_barrier(err.astype(jnp.bfloat16)).astype(jnp.float32)
            gu = jnp.einsum('tab,tbk->tak', errb, vrows)
            gv = jnp.einsum('tab,tak->tbk', errb, urows)
            grad_u = jnp.zeros((grid, TILE, RANK), jnp.float32).at[rows].add(gu)
            grad_v = jnp.zeros((grid, TILE, RANK), jnp.float32).at[cols].add(gv)
            return (sse, grad_u, grad_v)
        sse, grad_u, grad_v = lax.map(one, (ratings[:, stratum], codes, live, user_b, item_b))
        total_sse = jnp.sum(sse)
        total_count = jnp.sum(tile_count[:, stratum].astype(jnp.float32)) * float(TILE * TILE)
        precision = (1.0 + total_count / 2.0) / (1.0 + total_sse / 2.0)
        grad_u = grad_u.reshape(USERS, RANK)
        grad_v = grad_v.reshape(ITEMS, RANK)
        grad_w = lax.dot_general(side_features, offset, (((0,), (0,)), ((), ())), preferred_element_type=jnp.float32)
        new_users = users + step_size * (precision * grad_u - prior_prec * (users - mean)) + noise_scale * user_noise[stratum].astype(jnp.float32)
        new_items = items + step_size * (precision * grad_v - item_prec * items) + noise_scale * item_noise[stratum].astype(jnp.float32)
        weights = weights + rate * (prior_prec * grad_w - weight_decay * weights)
        users = new_users
        if stratum + 1 < STRATA:
            items = jnp.roll(new_items, USR_DEV, axis=0)
        else:
            items = new_items
    return (users, items, weights)
```

```python
import functools
import math

import jax
import jax.numpy as jnp
from jax import lax
from jax.experimental import pallas as pl
from jax.experimental.pallas import tpu as pltpu
from jax.sharding import Mesh
from jax.sharding import PartitionSpec as P

USER = ("user_0", "user_1", "user_2", "user_3")
MESH = pl.DeviceIdType.MESH
F32 = jnp.float32
BF16 = jnp.bfloat16

step_size = 0.01
prior_prec = 8.0
item_prec = 1.0
weight_decay = 1.0
rate_scale = 0.04


def nt(a, b):
    return lax.dot_general(a, b, (((1,), (1,)), ((), ())), preferred_element_type=F32)


def tn(a, b):
    return lax.dot_general(a, b, (((0,), (0,)), ((), ())), preferred_element_type=F32)


def kernel(
    dims,
    index_ref, count_ref, ratings_hbm, feat_hbm, users_hbm, items_hbm, weights_hbm, unoise_hbm, inoise_hbm,
    users_out, items_out, weights_out,
    ratings, feat, featT, users, items, new_items, w0, wb, unoise, inoise, mean, off, err_b, grad_u, grad_v,
    g_send, g_sum, core_in, plane_in, z_out, z_in, w_own, wz, wfull, pay, sse_plane, pay2, sse_z, fin, wout,
    load, store, core_s, core_r, prs_s, prs_r, zrs_s, zrs_r, zag_s, zag_r, pag_s, pag_r, fwd_s, fwd_r,
    sp_s, sp_r, sz_s, sz_r, sh_s, sh_r, fin_s, fin_r,
):
    NZ, NX, NY, strata, slots, tile, rows, featn, rank = dims
    NP = NX * NY
    half = rank // 2
    grid = rows // tile
    T2 = NZ // 2
    rate = rate_scale / (rows * NZ * NP * 2)
    noise_scale = math.sqrt(2.0 * step_size)

    z = lax.axis_index("user_0")
    x = lax.axis_index("user_1")
    y = lax.axis_index("user_2")
    c = lax.axis_index("user_3")
    p = x * NY + y
    par = lax.rem(y, 2)
    pp = p // 2
    owner = lax.rem(z + y, 2) == 0
    partner = (z, x, y, 1 - c)

    def plane_peer(i):
        return lax.rem(x + i // NY, NX), lax.rem(y + lax.rem(i, NY), NY)

    def device_of(idx):
        cc = lax.rem(idx, 2)
        k = idx // 2
        yy = lax.rem(k, NY)
        k = k // NY
        return (k // NX, lax.rem(k, NX), yy, cc)

    total = NZ * NP * 2
    me = (z * NP + p) * 2 + c
    nxt = device_of(lax.rem(me + 1, total))
    prv = device_of(lax.rem(me + total - 1, total))

    def bytes_wait(ref, sem):
        pltpu.make_async_copy(ref, ref, sem).wait()

    def remote(src, dst, s_sem, r_sem, dev):
        return pltpu.make_async_remote_copy(src_ref=src, dst_ref=dst, send_sem=s_sem, recv_sem=r_sem,
                                            device_id=dev, device_id_type=MESH)

    pairs = ((feat_hbm, feat), (weights_hbm, w0), (users_hbm, users), (items_hbm, items.at[0]),
             (ratings_hbm.at[0], ratings), (unoise_hbm, unoise), (inoise_hbm, inoise))
    loads = [pltpu.make_async_copy(a, b, load.at[i]) for i, (a, b) in enumerate(pairs)]
    for cp in loads:
        cp.start()

    barrier = pltpu.get_barrier_semaphore()

    def hello(dev):
        pl.semaphore_signal(barrier, inc=1, device_id=dev, device_id_type=MESH)

    def hello_plane(i, _):
        xx, yy = plane_peer(i)
        hello((z, xx, yy, c))
        hello((z, xx, yy, 1 - c))
        return 0

    def hello_z(i, _):
        hello((lax.rem(z + i, NZ), x, y, c))
        return 0

    hello(partner)
    hello(nxt)
    hello(prv)
    lax.fori_loop(1, NP, hello_plane, 0)
    lax.fori_loop(1, NZ, hello_z, 0)

    def tile_pass(s):
        ub = users[...].astype(BF16)
        hb = items[s].astype(BF16)
        count = count_ref[0, s]
        sse = jnp.zeros((1, tile), F32)
        for r in range(grid):
            pred = nt(ub[r * tile:(r + 1) * tile], hb)
            parts = []
            for col in range(grid):
                k = r * grid + col
                slot = jnp.int32(0)
                live = jnp.float32(0.0)
                for t in range(slots):
                    hit = index_ref[0, s, t] == k
                    slot = jnp.where(hit, jnp.int32(t), slot)
                    live = jnp.where(jnp.logical_and(hit, t < count), jnp.float32(1.0), live)
                e = live * (ratings[s, slot].astype(F32) - pred[:, col * tile:(col + 1) * tile])
                sse = sse + jnp.sum(e * e, axis=0, keepdims=True)
                parts.append(e.astype(BF16))
            row = jnp.concatenate(parts, axis=1)
            err_b[r * tile:(r + 1) * tile, :] = row
            grad_u[r * tile:(r + 1) * tile, :] = jnp.dot(row, hb, preferred_element_type=F32)
        grad_v[...] = tn(err_b[...], ub)
        pay[s, 0:1, :] = sse
        pay[s, 1:2, :] = jnp.broadcast_to(count.astype(F32) * float(tile * tile) / float(tile), (1, tile))

    def sse_plane_send(s):
        slot = p * 2 + c
        dst = sse_plane.at[s, slot]
        remote(pay.at[s], dst, sp_s.at[s], sp_r.at[s], partner).start()

        def body(i, _):
            xx, yy = plane_peer(i)
            remote(pay.at[s], dst, sp_s.at[s], sp_r.at[s], (z, xx, yy, c)).start()
            remote(pay.at[s], dst, sp_s.at[s], sp_r.at[s], (z, xx, yy, 1 - c)).start()
            return 0

        lax.fori_loop(1, NP, body, 0)
        sse_plane[s, slot] = pay[s]

    def sse_z_send(s):
        bytes_wait(sse_plane.at[s, pl.ds(0, 2 * NP - 1)], sp_r.at[s])
        tot = jnp.sum(sse_plane[s], axis=0)
        pay2[s] = tot
        sse_z[s, z] = tot

        def body(i, _):
            remote(pay2.at[s], sse_z.at[s, z], sz_s.at[s], sz_r.at[s], (lax.rem(z + i, NZ), x, y, c)).start()
            return 0

        lax.fori_loop(1, NZ, body, 0)

    def update(s, dst_items):
        bytes_wait(sse_z.at[s, pl.ds(0, NZ - 1)], sz_r.at[s])
        tot = jnp.sum(sse_z[s], axis=0)
        sums = jnp.sum(tot, axis=1, keepdims=True)
        precision = (1.0 + sums[1:2, :] / 2.0) / (1.0 + sums[0:1, :] / 2.0)
        pr = jnp.broadcast_to(precision, (1, rank))
        if s == 0:
            loads[6].wait()
            loads[5].wait()
        h = items[s]
        dst_items[...] = (h + step_size * (pr * grad_v[...] - item_prec * h)
                          + noise_scale * inoise[s].astype(F32))
        if s + 1 < strata:
            remote(new_items.at[s], items.at[s + 1], sh_s.at[s], sh_r.at[s], nxt).start()
        u = users[...]
        users[...] = (u + step_size * (pr * grad_u[...] - prior_prec * (u - mean[...]))
                      + noise_scale * unoise[s].astype(F32))

    for s in range(strata):
        last = s + 1 == strata
        if s == 0:
            loads[0].wait()
            loads[1].wait()
            wb[...] = w0[...].astype(BF16)
            for i in range(rows // 128):
                featT[:, i * 128:(i + 1) * 128] = feat[i * 128:(i + 1) * 128, :].T
            t_own = z * (NP // 2) + pp
            own8 = w0[pl.ds(pl.multiple_of(t_own * 8, 8), 8), :]
            w_own[...] = jnp.where(c == 0, own8[:, :half], own8[:, half:])
        mean[...] = jnp.dot(feat[...], wb[...], preferred_element_type=F32)
        if s == 0:
            loads[2].wait()
        o = (users[...] - mean[...]).astype(BF16)
        off[0] = o[:, :half]
        off[1] = o[:, half:]
        if s > 0:
            bytes_wait(g_send, core_s.at[s - 1])
        g_send[...] = jnp.dot(featT[...], off[1 - c], preferred_element_type=F32).reshape(g_send.shape)
        if s == 0:
            pl.semaphore_wait(barrier, 2 * (NP - 1) + NZ - 1 + 3)
        remote(g_send, core_in.at[s], core_s.at[s], core_r.at[s], partner).start()
        if s > 0:
            bytes_wait(plane_in.at[s, pl.ds(0, NP - 1)], prs_s.at[s - 1])
        g_sum[...] = jnp.dot(featT[...], off[c], preferred_element_type=F32).reshape(g_sum.shape)
        if s == 0:
            loads[3].wait()
            loads[4].wait()
            tile_pass(0)
            sse_plane_send(0)
        bytes_wait(core_in.at[s], core_r.at[s])
        g_sum[...] = g_sum[...] + core_in[s]

        def plane_send(i, _):
            xx, yy = plane_peer(NP - i)
            q = xx * NY + yy
            remote(g_sum.at[:, lax.rem(q, 2), q // 2], plane_in.at[s, p], prs_s.at[s], prs_r.at[s], (z, xx, yy, c)).start()
            return 0

        lax.fori_loop(1, NP, plane_send, 0)
        plane_in[s, p] = g_sum[:, par, pp]
        if s > 0:
            sse_z_send(s)
        bytes_wait(plane_in.at[s, pl.ds(0, NP - 1)], prs_r.at[s])
        acc = plane_in[s, 0]
        for q in range(1, NP):
            acc = acc + plane_in[s, q]
        if s > 0:
            @pl.when(owner)
            def _():
                bytes_wait(z_out.at[pl.ds(0, T2 - 1)], zrs_s.at[s - 1])

            @pl.when(jnp.logical_not(owner))
            def _():
                bytes_wait(z_out, zrs_s.at[s - 1])
        z_out[...] = acc
        shift = lax.rem(z + y, 2)

        def z_send(i, _):
            zz = lax.rem(z + shift + 2 * i, NZ)

            @pl.when(zz != z)
            def _():
                remote(z_out.at[zz // 2], z_in.at[s, z], zrs_s.at[s], zrs_r.at[s], (zz, x, y, c)).start()

            return 0

        lax.fori_loop(0, T2, z_send, 0)
        if s == 0:
            sse_z_send(0)

        @pl.when(owner)
        def _():
            z_in[s, z] = z_out[z // 2]
            bytes_wait(z_in.at[s, pl.ds(0, NZ - 1)], zrs_r.at[s])
            g = z_in[s, 0]
            for k in range(1, NZ):
                g = g + z_in[s, k]
            w = w_own[...]
            w = w + rate * (prior_prec * g - weight_decay * w)
            w_own[...] = w
            if last:
                fin[c] = w
                for n, dev in enumerate((partner, (z, x, y + 1 - 2 * par, c), (z, x, y + 1 - 2 * par, 1 - c))):
                    remote(w_own, fin.at[c], fin_s.at[n], fin_r.at[c], dev).start()
            else:
                wz[s, z // 2] = w

                def ag_send(i, _):
                    remote(wz.at[s, z // 2], wz.at[s, z // 2], zag_s.at[s], zag_r.at[s], (lax.rem(z + i, NZ), x, y, c)).start()
                    return 0

                lax.fori_loop(1, NZ, ag_send, 0)

        if last:
            update(s, new_items.at[s])
            st = [pltpu.make_async_copy(users, users_out, store.at[0]),
                  pltpu.make_async_copy(new_items.at[s], items_out, store.at[1])]
            for cp in st:
                cp.start()

            @pl.when(owner)
            def _():
                bytes_wait(fin.at[0], fin_r.at[1 - c])

            @pl.when(jnp.logical_not(owner))
            def _():
                bytes_wait(fin.at[0], fin_r.at[0])
                bytes_wait(fin.at[1], fin_r.at[1])

            r0 = par * 4 + c * 2
            for h in range(2):
                t8 = fin[h]
                o2 = t8[0:2]
                for k in range(1, 4):
                    o2 = jnp.where(r0 == 2 * k, t8[2 * k:2 * k + 2], o2)
                wout[:, h * half:(h + 1) * half] = o2
            cp = pltpu.make_async_copy(wout, weights_out, store.at[2])
            cp.start()
            for d in (*st, cp):
                d.wait()
        else:
            update(s, new_items.at[s])

            @pl.when(owner)
            def _():
                bytes_wait(wz.at[s, pl.ds(0, T2 - 1)], zag_r.at[s])

            @pl.when(jnp.logical_not(owner))
            def _():
                bytes_wait(wz.at[s], zag_r.at[s])

            def pag_send(i, _):
                xx, yy = plane_peer(NP - i)
                remote(wz.at[s], wfull.at[s, c, :, par, pp], pag_s.at[s], pag_r.at[s, p], (z, xx, yy, c)).start()
                return 0

            lax.fori_loop(1, NP, pag_send, 0)
            remote(wz.at[s], wfull.at[s, c, :, par, pp], fwd_s.at[s], fwd_r.at[s], partner).start()
            wfull[s, c, :, par, pp] = wz[s]
            bytes_wait(items.at[s + 1], sh_r.at[s])
            bytes_wait(new_items.at[s], sh_s.at[s])
            tile_pass(s + 1)
            sse_plane_send(s + 1)

            def forward(i, _):
                xx, yy = plane_peer(i)
                q = xx * NY + yy
                piece = wfull.at[s, c, :, lax.rem(q, 2), q // 2]
                bytes_wait(piece, pag_r.at[s, q])
                remote(piece, piece, fwd_s.at[s], fwd_r.at[s], partner).start()
                return 0

            lax.fori_loop(1, NP, forward, 0)
            bytes_wait(wfull.at[s, 1 - c], fwd_r.at[s])
            wb[:, :half] = wfull[s, 0].reshape(featn, half).astype(BF16)
            wb[:, half:] = wfull[s, 1].reshape(featn, half).astype(BF16)

    e = strata - 1
    bytes_wait(g_send, core_s.at[e])
    bytes_wait(plane_in.at[e, pl.ds(0, NP - 1)], prs_s.at[e])

    @pl.when(owner)
    def _():
        bytes_wait(z_out.at[pl.ds(0, T2 - 1)], zrs_s.at[e])
        for s in range(e):
            bytes_wait(z_in.at[s, pl.ds(0, NZ - 1)], zag_s.at[s])
        bytes_wait(core_in.at[e, 0, 0, pl.ds(0, 1)], fin_s.at[0])
        bytes_wait(core_in.at[e, 0, 0, pl.ds(0, 1)], fin_s.at[1])
        bytes_wait(core_in.at[e, 0, 0, pl.ds(0, 1)], fin_s.at[2])

    @pl.when(jnp.logical_not(owner))
    def _():
        bytes_wait(z_out, zrs_s.at[e])

    for s in range(strata):
        bytes_wait(sse_plane.at[s, pl.ds(0, 2 * NP - 1)], sp_s.at[s])
        bytes_wait(sse_z.at[s, pl.ds(0, NZ - 1)], sz_s.at[s])
        if s < e:
            bytes_wait(plane_in.at[s, pl.ds(0, NP - 1)], pag_s.at[s])
            bytes_wait(wfull.at[s, c], fwd_s.at[s])


def local(ratings, tile_index, tile_count, side, users, items, weights, unoise, inoise):
    nz, nx, ny = (lax.axis_size(a) for a in USER[:3])
    strata, slots, tile = ratings.shape[1:4]
    rows, rank = users.shape
    featn = side.shape[1]
    npl, t2, half = nx * ny, nz // 2, rank // 2
    dims = (nz, nx, ny, strata, slots, tile, rows, featn, rank)
    g_shape = (t2, 2, npl // 2, 8, half)
    V, D = pltpu.VMEM, pltpu.SemaphoreType.DMA
    data = [
        V((strata, slots, tile, tile), BF16),
        V((rows, featn), BF16),
        V((featn, rows), BF16),
        V((rows, rank), F32),
        V((strata, rows, rank), F32),
        V((strata, rows, rank), F32),
        V((featn, rank), F32),
        V((featn, rank), BF16),
        V((strata, rows, rank), BF16),
        V((strata, rows, rank), BF16),
        V((rows, rank), F32),
        V((2, rows, half), BF16),
        V((rows, rows), BF16),
        V((rows, rank), F32),
        V((rows, rank), F32),
        V(g_shape, F32),
        V(g_shape, F32),
        V((strata, *g_shape), F32),
        V((strata, npl, t2, 8, half), F32),
        V((t2, 8, half), F32),
        V((strata, nz, 8, half), F32),
        V((8, half), F32),
        V((strata - 1, t2, 8, half), F32),
        V((strata - 1, 2, *g_shape), F32),
        V((strata, 2, tile), F32),
        V((strata, 2 * npl, 2, tile), F32),
        V((strata, 2, tile), F32),
        V((strata, nz, 2, tile), F32),
        V((2, 8, half), F32),
        V((2, rank), F32),
    ]
    sems = [
        D((7,)), D((3,)),
        D((strata,)), D((strata,)),
        D((strata,)), D((strata,)),
        D((strata,)), D((strata,)),
        D((strata,)), D((strata,)),
        D((strata,)), D((strata, npl)),
        D((strata,)), D((strata,)),
        D((strata,)), D((strata,)),
        D((strata,)), D((strata,)),
        D((strata,)), D((strata,)),
        D((3,)), D((2,)),
    ]
    any_ = pl.BlockSpec(memory_space=pl.ANY)
    smem = pl.BlockSpec(memory_space=pltpu.SMEM)
    return pl.pallas_call(
        functools.partial(kernel, dims),
        out_shape=(
            jax.ShapeDtypeStruct((rows, rank), F32),
            jax.ShapeDtypeStruct((rows, rank), F32),
            jax.ShapeDtypeStruct((2, rank), F32),
        ),
        in_specs=[smem, smem] + [any_] * 7,
        out_specs=(any_, any_, any_),
        scratch_shapes=data + sems,
        compiler_params=pltpu.CompilerParams(collective_id=0, has_side_effects=True),
        name="sweep",
    )(tile_index, tile_count, ratings, side, users, items, weights, unoise, inoise)


def finer_of(mesh):
    return Mesh(mesh.devices.reshape(16, 4, 4, 2), USER)


def solution(mesh):
    return over(finer_of(mesh))


def over(finer):
    return jax.shard_map(
        local,
        mesh=finer,
        in_specs=(
            P(USER, None, None, None, None),
            P(USER, None, None),
            P(USER, None),
            P(USER, None),
            P(USER, None),
            P(USER, None),
            P(),
            P(None, USER, None),
            P(None, USER, None),
        ),
        out_specs=(P(USER, None), P(USER, None), P(USER, None)),
        check_vma=False,
    )
```

```python
import functools
import math

import jax
import jax.numpy as jnp
from jax import lax
from jax.experimental import pallas as pl
from jax.experimental.pallas import tpu as pltpu
from jax.sharding import Mesh
from jax.sharding import PartitionSpec as P

USER = ("user_0", "user_1", "user_2", "user_3")
MESH = pl.DeviceIdType.MESH
F32 = jnp.float32
BF16 = jnp.bfloat16

step_size = 0.01
prior_prec = 8.0
item_prec = 1.0
weight_decay = 1.0
rate_scale = 0.04


def nt(a, b):
    return lax.dot_general(a, b, (((1,), (1,)), ((), ())), preferred_element_type=F32)


def tn(a, b):
    return lax.dot_general(a, b, (((0,), (0,)), ((), ())), preferred_element_type=F32)


def kernel(
    dims,
    index_ref, count_ref, ratings_hbm, feat_hbm, users_hbm, items_hbm, weights_hbm, unoise_hbm, inoise_hbm,
    users_out, items_out, weights_out,
    ratings, feat, featT, feat_out, feat_in, users, users_in, items, new_items, w0, wb, unoise, inoise, mean, mean_send,
    off, err_b, grad_u, grad_v, ce_send, ce_in, g_sum, plane_in, z_out, z_in, w_own, wz, wfull,
    pay, sse_plane, pay2, sse_z, fin,
    load, ce_s, ce_r, fx_s, fx_r, ux_s, ux_r, mx_s, mx_r, prs_s, prs_r, zrs_s, zrs_r,
    zag_s, zag_r, pag_s, pag_r, sp_s, sp_r, sz_s, sz_r, sh_s, sh_r, fin_s, fin_r, met,
):
    NZ, NX, NY, strata, slots, tile, rows, featn, rank = dims
    NP = NX * NY
    half = rank // 2
    grid = rows // tile
    T2 = NZ // 2
    R8 = featn // (T2 * NP)
    jobs = 3
    pairs_z = T2 // 2
    span = featn // T2
    rate = rate_scale / (rows * NZ * NP * 2)
    noise_scale = math.sqrt(2.0 * step_size)

    z = lax.axis_index("user_0")
    x = lax.axis_index("user_1")
    y = lax.axis_index("user_2")
    c = lax.axis_index("user_3")
    p = x * NY + y
    par = lax.rem(y, 2)
    yh = y // 2
    owner = lax.rem(z + y, 2) == 0
    other = jnp.logical_not(owner)
    partner = (z, x, y, 1 - c)

    def plane_peer(i):
        return lax.rem(x + i // NY, NX), lax.rem(y + lax.rem(i, NY), NY)

    xs = [lax.rem(x + d, NX) for d in range(NX)]
    ys = [lax.rem(y + d, NY) for d in range(NY)]
    yhs = [v // 2 for v in ys]
    pars = [par, 1 - par]
    order = sorted(((dx, dy) for dx in range(NX) for dy in range(NY) if dx or dy),
                   key=lambda d: -min(d[0], NX - d[0]) - min(d[1], NY - d[1]))
    peers = [(xs[dx], ys[dy], dy % 2, yhs[dy]) for dx, dy in order]

    def device_of(idx):
        cc = lax.rem(idx, 2)
        k = idx // 2
        yy = lax.rem(k, NY)
        k = k // NY
        return (k // NX, lax.rem(k, NX), yy, cc)

    total = NZ * NP * 2
    me = (z * NP + p) * 2 + c
    nxt = device_of(lax.rem(me + 1, total))
    prv = device_of(lax.rem(me + total - 1, total))

    share = plane_in.at[0, :, pl.ds(0, NP - 1)]

    def bytes_wait(ref, sem):
        pltpu.make_async_copy(ref, ref, sem).wait()

    def remote(src, dst, s_sem, r_sem, dev):
        return pltpu.make_async_remote_copy(src_ref=src, dst_ref=dst, send_sem=s_sem, recv_sem=r_sem,
                                            device_id=dev, device_id_type=MESH)

    pairs = ((feat_hbm, feat.at[pl.ds(0, rows)]), (weights_hbm, w0),
             (users_hbm.at[:, pl.ds(0, half)], users.at[0, 0]), (users_hbm.at[:, pl.ds(half, half)], users.at[0, 1]),
             (items_hbm, items.at[0]), (ratings_hbm.at[0], ratings), (unoise_hbm, unoise), (inoise_hbm, inoise))
    loads = [pltpu.make_async_copy(a, b, load.at[i]) for i, (a, b) in enumerate(pairs)]
    for cp in loads[:4]:
        cp.start()

    barrier = pltpu.get_barrier_semaphore()

    def hello(dev):
        pl.semaphore_signal(barrier, inc=1, device_id=dev, device_id_type=MESH)

    def hello_plane(i, _):
        xx, yy = plane_peer(i)
        hello((z, xx, yy, c))
        hello((z, xx, yy, 1 - c))
        return 0

    def hello_z(i, _):
        hello((lax.rem(z + i, NZ), x, y, c))
        return 0

    reach = NZ // 4
    far_z = 2 * reach < NZ - 1
    for dz in range(reach, 0, -1):
        hello_z(dz, 0)
        hello_z(NZ - dz, 0)
    n_hello = 2 * (NP - 1) + 2 * reach + 3
    lax.fori_loop(1, NP, hello_plane, 0)
    hello(partner)
    hello(nxt)
    hello(prv)
    for cp in loads[4:]:
        cp.start()

    def tile_pass(s):
        ub = jnp.concatenate([users[s, 0].astype(BF16), users[s, 1].astype(BF16)], axis=1)
        hb = items[s].astype(BF16)
        count = count_ref[0, s]
        sse = jnp.zeros((1, tile), F32)
        for r in range(grid):
            pred = nt(ub[r * tile:(r + 1) * tile], hb)
            parts = []
            for col in range(grid):
                k = r * grid + col
                slot = jnp.int32(0)
                live = jnp.float32(0.0)
                for t in range(slots):
                    hit = index_ref[s, 0, t] == k
                    slot = jnp.where(hit, jnp.int32(t), slot)
                    live = jnp.where(jnp.logical_and(hit, t < count), jnp.float32(1.0), live)
                e = live * (ratings[s, slot].astype(F32) - pred[:, col * tile:(col + 1) * tile])
                sse = sse + jnp.sum(e * e, axis=0, keepdims=True)
                parts.append(e.astype(BF16))
            row = jnp.concatenate(parts, axis=1)
            err_b[r * tile:(r + 1) * tile, :] = row
            grad_u[r * tile:(r + 1) * tile, :] = jnp.dot(row, hb, preferred_element_type=F32)
        grad_v[...] = tn(err_b[...], ub)
        pay[s, 0:1, :] = sse
        pay[s, 1:2, :] = jnp.broadcast_to(count.astype(F32) * float(tile * tile) / float(tile), (1, tile))

    def sse_z_send(s):
        def body(i, _):
            remote(pay.at[s], sse_z.at[s, z], sz_s.at[s], sz_r.at[s], (lax.rem(z + i, NZ), x, y, c)).start()
            return 0

        lax.fori_loop(1, NZ, body, 0)
        sse_z[s, z] = pay[s]

    def sse_plane_send(s):
        bytes_wait(sse_z.at[s, pl.ds(0, NZ - 1)], sz_r.at[s])
        tot = jnp.sum(sse_z[s], axis=0)
        pay2[s] = tot
        slot = p * 2 + c
        dst = sse_plane.at[s, slot]
        sse_plane[s, slot] = tot
        for xx, yy, d, yyh in peers:
            for cc in (c, 1 - c):
                remote(pay2.at[s], dst, sp_s.at[s], sp_r.at[s], (z, xx, yy, cc)).start()
        remote(pay2.at[s], dst, sp_s.at[s], sp_r.at[s], partner).start()

    def precision_of(s):
        bytes_wait(sse_plane.at[s, pl.ds(0, 2 * NP - 1)], sp_r.at[s])
        tot = jnp.sum(sse_plane[s], axis=0)
        sums = jnp.sum(tot, axis=1, keepdims=True)
        return (1.0 + sums[1:2, :] / 2.0) / (1.0 + sums[0:1, :] / 2.0)

    def update_items(s, precision):
        h = items[s]
        dst = new_items.at[s] if s + 1 < strata else items_out
        dst[...] = (h + step_size * (jnp.broadcast_to(precision, (1, rank)) * grad_v[...] - item_prec * h)
                        + noise_scale * inoise[s].astype(F32))

    def shift(s):
        remote(new_items.at[s], items.at[s + 1], sh_s.at[s], sh_r.at[s], nxt).start()

    def update_users(s, precision):
        pr = jnp.broadcast_to(precision, (1, half))
        for h in range(2):
            u = users[s, h]
            cols = slice(h * half, (h + 1) * half)
            new = (u + step_size * (pr * grad_u[:, cols] - prior_prec * (u - mean[s, h]))
                   + noise_scale * unoise[s][:, cols].astype(F32))
            if s + 1 < strata:
                users[s + 1, h] = new
            else:
                users_out[:, cols] = new

    def users_to_partner(s):
        remote(users.at[s, 1 - c], users_in.at[s - 1], ux_s.at[s - 1], ux_r.at[s - 1], partner).start()

    odd = lax.rem(z, 2)

    def pair(j):
        up = T2 // 2 + j * (1 - 2 * odd)
        down = T2 // 2 - 1 - j + odd * (2 + 2 * j)
        return lax.rem(z // 2 + up, T2), lax.rem(z // 2 + down, T2)

    groups = [t for j in range(pairs_z) for t in pair(j)]

    def group(ref, t):
        return ref[pl.ds(pl.multiple_of(t * span, 128), span), :]

    def group_send(k, i, t):
        for xx, yy, d, yyh in peers:
            remote(g_sum.at[k, t, pars[d], xx, yyh], plane_in.at[k, i, p], prs_s.at[k], prs_r.at[k, i], (z, xx, yy, c)).start()
        plane_in[k, i, p] = g_sum[k, t, par, x, yh]

    def plane_sum_z_send(k):
        for i, t in enumerate(groups):
            bytes_wait(plane_in.at[k, i, pl.ds(0, NP - 1)], prs_r.at[k, i])
            acc = plane_in[k, i, 0]
            for q in range(1, NP):
                acc = acc + plane_in[k, i, q]
            z_out[k, i] = acc

            def send():
                remote(z_out.at[k, i], z_in.at[k, z], zrs_s.at[k], zrs_r.at[k], (2 * t + par, x, y, c)).start()

            if i == T2 - 1:
                pl.when(other)(send)
            else:
                send()

    def z_sum(k):
        z_in[k, z] = z_out[k, T2 - 1]
        bytes_wait(z_in.at[k, pl.ds(0, NZ - 1)], zrs_r.at[k])
        g = z_in[k, 0]
        for n in range(1, NZ):
            g = g + z_in[k, n]
        return g

    def step_weights(g):
        w = w_own[...]
        w = w + rate * (prior_prec * g - weight_decay * w)
        w_own[...] = w
        return w

    def weights_along_z(s):
        @pl.when(owner)
        def _():
            wz[s, z // 2] = step_weights(z_sum(s))

            def body(i, _):
                for d in (T2 - i, T2 + i):
                    remote(wz.at[s, z // 2], wz.at[s, z // 2], zag_s.at[s], zag_r.at[s, z // 2],
                           (lax.rem(z + d, NZ), x, y, c)).start()
                return 0

            remote(wz.at[s, z // 2], wz.at[s, z // 2], zag_s.at[s], zag_r.at[s, z // 2],
                   (lax.rem(z + T2, NZ), x, y, c)).start()
            lax.fori_loop(1, T2, body, 0)

    def weights_over_plane(s):
        for j in range(pairs_z - 1, -1, -1):
            for n, t in reversed(tuple(enumerate(pair(j)))):
                def arrived():
                    bytes_wait(wz.at[s, t], zag_r.at[s, t])

                if j == pairs_z - 1 and n == 1:
                    pl.when(other)(arrived)
                else:
                    arrived()
                for xx, yy, d, yyh in peers:
                    remote(wz.at[s, t], wfull.at[s, t, par, x, yh], pag_s.at[s], pag_r.at[s, j], (z, xx, yy, c)).start()
                wfull[s, t, par, x, yh] = wz[s, t]

    def mean_of_both(s):
        acc = None
        for j in range(pairs_z - 1, -1, -1):
            bytes_wait(share.at[pl.ds(0, 2)], pag_r.at[s, j])
            t0, t1 = pair(j)
            w = jnp.concatenate([wfull[s, t].reshape(span, half).astype(BF16) for t in (t0, t1)], axis=0)
            f = jnp.concatenate([feat[:, pl.ds(pl.multiple_of(t * span, 128), span)] for t in (t0, t1)], axis=1)
            part = jnp.dot(f, w, preferred_element_type=F32)
            acc = part if acc is None else acc + part
        return acc

    def means_to_partner(s, m):
        mean_send[s - 1] = m[rows:]
        remote(mean_send.at[s - 1], mean.at[s, c], mx_s.at[s - 1], mx_r.at[s - 1], partner).start()

    loads[0].wait()
    loads[1].wait()
    wb[...] = w0[...].astype(BF16)
    for i in range(rows // 128):
        featT[:, i * 128:(i + 1) * 128] = feat[i * 128:(i + 1) * 128, :].T
    t_own = z * (NP // 2) + p // 2
    own8 = w0[pl.ds(pl.multiple_of(t_own * R8, 8), R8), :]
    w_own[...] = jnp.where(c == 0, own8[:, :half], own8[:, half:])
    m = jnp.dot(feat[0:rows], wb[...], preferred_element_type=F32)
    loads[2].wait()
    loads[3].wait()
    for h in range(2):
        mh = m[:, h * half:(h + 1) * half]
        mean[0, h] = mh
        off[h] = (users[0, h] - mh).astype(BF16)
    shape = ce_send.shape[1:]
    for i, t in enumerate(groups):
        ce_send[t] = jnp.dot(group(featT, t)[:, 0:rows], off[1 - c], preferred_element_type=F32).reshape(shape)
        if i == 0:
            pl.semaphore_wait(barrier, n_hello)
            if far_z:
                for dz in (reach, NZ - reach):
                    pl.semaphore_signal(met, inc=1, device_id=(lax.rem(z + dz, NZ), x, y, c), device_id_type=MESH)
        remote(ce_send.at[t], ce_in.at[t], ce_s, ce_r.at[i], partner).start()
    for i, t in enumerate(groups):
        g = jnp.dot(group(featT, t)[:, 0:rows], off[c], preferred_element_type=F32).reshape(shape)
        bytes_wait(ce_in.at[t], ce_r.at[i])
        g_sum[0, t] = g + ce_in[t]
        group_send(0, i, t)
    loads[4].wait()
    loads[5].wait()
    tile_pass(0)
    if far_z:
        pl.semaphore_wait(met, 2)
    sse_z_send(0)
    feat_out[...] = feat[0:rows].astype(F32)
    remote(feat_out, feat_in, fx_s, fx_r, partner).start()
    plane_sum_z_send(0)
    sse_plane_send(0)
    bytes_wait(feat_in, fx_r)
    feat[rows:, :] = feat_in[...].astype(BF16)
    for i in range(rows // 128):
        featT[:, rows + i * 128:rows + (i + 1) * 128] = feat[rows + i * 128:rows + (i + 1) * 128, :].T
    for cp in loads[6:]:
        cp.wait()
    for s in range(strata - 1):
        weights_along_z(s)
        weights_over_plane(s)
        precision = precision_of(s)
        update_items(s, precision)
        shift(s)
        if s > 0:
            bytes_wait(mean.at[s, 0], mx_r.at[s - 1])
        update_users(s, precision)
        users_to_partner(s + 1)
        n = s + 1
        m = mean_of_both(s)
        bytes_wait(users_in.at[s], ux_r.at[s])
        o = jnp.concatenate([users[n, c] - m[:rows], users_in[s] - m[rows:]], axis=0).astype(BF16)

        def send_groups(some):
            for i in some:
                t = groups[i]
                g_sum[n, t] = jnp.dot(group(featT, t), o, preferred_element_type=F32).reshape(shape)
                group_send(n, i, t)

        send_groups(range(T2 // 2))
        bytes_wait(items.at[n], sh_r.at[s])
        tile_pass(n)
        sse_z_send(n)
        send_groups(range(T2 // 2, T2))
        mean[n, c] = m[:rows]
        means_to_partner(n, m)
        plane_sum_z_send(n)
        sse_plane_send(n)

    @pl.when(owner)
    def _():
        w = step_weights(z_sum(strata - 1))
        fin[c] = w
        for n, dev in enumerate((partner, (z, x, y + 1 - 2 * par, c), (z, x, y + 1 - 2 * par, 1 - c))):
            remote(w_own, fin.at[c], fin_s.at[n], fin_r.at[c], dev).start()

    e = strata - 1
    bytes_wait(mean.at[e, 0], mx_r.at[e - 1])
    precision = precision_of(e)
    update_items(e, precision)
    update_users(e, precision)

    @pl.when(owner)
    def _():
        bytes_wait(fin.at[0], fin_r.at[1 - c])

    @pl.when(other)
    def _():
        bytes_wait(fin.at[0], fin_r.at[0])
        bytes_wait(fin.at[1], fin_r.at[1])

    r2 = R8 // 4
    for h in range(2):
        t8 = fin[h]
        o2 = t8[0:r2]
        for k in range(1, 4):
            o2 = jnp.where(par * 2 + c == k, t8[r2 * k:r2 * (k + 1)], o2)
        weights_out[:, h * half:(h + 1) * half] = o2

    bytes_wait(ce_send, ce_s)
    bytes_wait(feat_out, fx_s)
    for s in range(strata - 1):
        bytes_wait(users_in.at[s], ux_s.at[s])
        bytes_wait(mean_send.at[s], mx_s.at[s])
        bytes_wait(new_items.at[s], sh_s.at[s])
        bytes_wait(share, pag_s.at[s])
    for k in range(jobs):
        bytes_wait(share, prs_s.at[k])

    @pl.when(owner)
    def _():
        for k in range(jobs):
            bytes_wait(z_out.at[k, pl.ds(0, T2 - 1)], zrs_s.at[k])
        for s in range(strata - 1):
            bytes_wait(z_in.at[s, pl.ds(0, NZ - 1)], zag_s.at[s])
        for n in range(3):
            bytes_wait(w_own, fin_s.at[n])

    @pl.when(other)
    def _():
        for k in range(jobs):
            bytes_wait(z_out.at[k], zrs_s.at[k])

    for s in range(strata):
        bytes_wait(sse_plane.at[s, pl.ds(0, 2 * NP - 1)], sp_s.at[s])
        bytes_wait(sse_z.at[s, pl.ds(0, NZ - 1)], sz_s.at[s])


def local(ratings, tile_index, tile_count, side, users, items, weights, unoise, inoise):
    nz, nx, ny = (lax.axis_size(a) for a in USER[:3])
    strata, slots, tile = ratings.shape[1:4]
    rows, rank = users.shape
    featn = side.shape[1]
    npl, t2, half = nx * ny, nz // 2, rank // 2
    r8 = featn // (t2 * npl)
    jobs = 3
    dims = (nz, nx, ny, strata, slots, tile, rows, featn, rank)
    g_shape = (t2, 2, nx, ny // 2, r8, half)
    V, D = pltpu.VMEM, pltpu.SemaphoreType.DMA
    data = [
        V((strata, slots, tile, tile), BF16),
        V((2 * rows, featn), BF16),
        V((featn, 2 * rows), BF16),
        V((rows, featn), F32),
        V((rows, featn), F32),
        V((strata, 2, rows, half), F32),
        V((strata - 1, rows, half), F32),
        V((strata, rows, rank), F32),
        V((strata - 1, rows, rank), F32),
        V((featn, rank), F32),
        V((featn, rank), BF16),
        V((strata, rows, rank), BF16),
        V((strata, rows, rank), BF16),
        V((strata, 2, rows, half), F32),
        V((strata - 1, rows, half), F32),
        V((2, rows, half), BF16),
        V((rows, rows), BF16),
        V((rows, rank), F32),
        V((rows, rank), F32),
        V(g_shape, F32),
        V(g_shape, F32),
        V((jobs, *g_shape), F32),
        V((jobs, t2, npl, r8, half), F32),
        V((jobs, t2, r8, half), F32),
        V((jobs, nz, r8, half), F32),
        V((r8, half), F32),
        V((strata - 1, t2, r8, half), F32),
        V((strata - 1, *g_shape), F32),
        V((strata, 2, tile), F32),
        V((strata, 2 * npl, 2, tile), F32),
        V((strata, 2, tile), F32),
        V((strata, nz, 2, tile), F32),
        V((2, r8, half), F32),
    ]
    sems = [
        D((8,)),
        D(()), D((t2,)),
        D(()), D(()),
        D((strata - 1,)), D((strata - 1,)),
        D((strata - 1,)), D((strata - 1,)),
        D((jobs,)), D((jobs, t2)),
        D((jobs,)), D((jobs,)),
        D((strata - 1,)), D((strata - 1, t2)),
        D((strata - 1,)), D((strata - 1, t2 // 2)),
        D((strata,)), D((strata,)),
        D((strata,)), D((strata,)),
        D((strata - 1,)), D((strata - 1,)),
        D((3,)), D((2,)),
        pltpu.SemaphoreType.REGULAR,
    ]
    any_ = pl.BlockSpec(memory_space=pltpu.HBM)
    vmem = pl.BlockSpec(memory_space=pltpu.VMEM)
    smem = pl.BlockSpec(memory_space=pltpu.SMEM)
    return pl.pallas_call(
        functools.partial(kernel, dims),
        out_shape=(
            jax.ShapeDtypeStruct((rows, rank), F32),
            jax.ShapeDtypeStruct((rows, rank), F32),
            jax.ShapeDtypeStruct((r8 // 4, rank), F32),
        ),
        in_specs=[smem, smem] + [any_] * 7,
        out_specs=(vmem, vmem, vmem),
        scratch_shapes=data + sems,
        compiler_params=pltpu.CompilerParams(collective_id=0, has_side_effects=True, vmem_limit_bytes=53 * 1024 * 1024),
        name="sweep",
    )(jnp.transpose(tile_index, (1, 0, 2)), tile_count, ratings, side, users, items, weights, unoise, inoise)


def finer_of(mesh):
    return Mesh(mesh.devices.reshape(16, 4, 4, 2), USER)


def solution(mesh):
    return over(finer_of(mesh))


def over(finer):
    return jax.shard_map(
        local,
        mesh=finer,
        in_specs=(
            P(USER, None, None, None, None),
            P(USER, None, None),
            P(USER, None),
            P(USER, None),
            P(USER, None),
            P(USER, None),
            P(),
            P(None, USER, None),
            P(None, USER, None),
        ),
        out_specs=(P(USER, None), P(USER, None), P(USER, None)),
        check_vma=False,
    )
```

```python
import functools
import math

import jax
import jax.numpy as jnp
from jax import lax
from jax.experimental import pallas as pl
from jax.experimental.pallas import tpu as pltpu
from jax.sharding import Mesh
from jax.sharding import PartitionSpec as P

USER = ("user_0", "user_1", "user_2", "user_3")
MESH = pl.DeviceIdType.MESH
F32 = jnp.float32
BF16 = jnp.bfloat16

step_size = 0.01
prior_prec = 8.0
item_prec = 1.0
weight_decay = 1.0
rate_scale = 0.04


def nt(a, b):
    return lax.dot_general(a, b, (((1,), (1,)), ((), ())), preferred_element_type=F32)


def tn(a, b):
    return lax.dot_general(a, b, (((0,), (0,)), ((), ())), preferred_element_type=F32)


def kernel(
    dims,
    index_ref, count_ref, ratings_hbm, feat_hbm, users_hbm, items_hbm, weights_hbm, unoise_hbm, inoise_hbm,
    users_out, items_out, weights_out,
    ratings, feat, featT, feat_out, feat_in, users, users_in, items, new_items, w0, wb, unoise, inoise, mean, mean_send,
    off, err_b, grad_u, grad_v, ce_send, ce_in, g_sum, plane_in, z_out, z_in, w_own, wz, wfull,
    pay, sse_plane, pay2, sse_z, fin,
    load, ce_s, ce_r, fx_s, fx_r, ux_s, ux_r, mx_s, mx_r, prs_s, prs_r, zrs_s, zrs_r,
    zag_s, zag_r, pag_s, pag_r, sp_s, sp_r, sz_s, sz_r, sh_s, sh_r, fin_s, fin_r, met,
):
    NZ, NX, NY, strata, slots, tile, rows, featn, rank = dims
    NP = NX * NY
    half = rank // 2
    grid = rows // tile
    T2 = NZ // 2
    R8 = featn // (T2 * NP)
    jobs = 3
    pairs_z = T2 // 2
    span = featn // T2
    rate = rate_scale / (rows * NZ * NP * 2)
    noise_scale = math.sqrt(2.0 * step_size)

    z = lax.axis_index("user_0")
    x = lax.axis_index("user_1")
    y = lax.axis_index("user_2")
    c = lax.axis_index("user_3")
    p = x * NY + y
    par = lax.rem(y, 2)
    yh = y // 2
    owner = lax.rem(z + y, 2) == 0
    other = jnp.logical_not(owner)
    partner = (z, x, y, 1 - c)

    def plane_peer(i):
        return lax.rem(x + i // NY, NX), lax.rem(y + lax.rem(i, NY), NY)

    xs = [lax.rem(x + d, NX) for d in range(NX)]
    ys = [lax.rem(y + d, NY) for d in range(NY)]
    yhs = [v // 2 for v in ys]
    pars = [par, 1 - par]
    order = sorted(((dx, dy) for dx in range(NX) for dy in range(NY) if dx or dy),
                   key=lambda d: -min(d[0], NX - d[0]) - min(d[1], NY - d[1]))
    peers = [(xs[dx], ys[dy], dy % 2, yhs[dy]) for dx, dy in order]

    def device_of(idx):
        cc = lax.rem(idx, 2)
        k = idx // 2
        yy = lax.rem(k, NY)
        k = k // NY
        return (k // NX, lax.rem(k, NX), yy, cc)

    total = NZ * NP * 2
    me = (z * NP + p) * 2 + c
    nxt = device_of(lax.rem(me + 1, total))
    prv = device_of(lax.rem(me + total - 1, total))

    share = plane_in.at[0, :, pl.ds(0, NP - 1)]

    def bytes_wait(ref, sem):
        pltpu.make_async_copy(ref, ref, sem).wait()

    def remote(src, dst, s_sem, r_sem, dev):
        return pltpu.make_async_remote_copy(src_ref=src, dst_ref=dst, send_sem=s_sem, recv_sem=r_sem,
                                            device_id=dev, device_id_type=MESH)

    pairs = ((feat_hbm, feat.at[pl.ds(0, rows)]), (weights_hbm, w0),
             (users_hbm.at[:, pl.ds(0, half)], users.at[0, 0]), (users_hbm.at[:, pl.ds(half, half)], users.at[0, 1]),
             (items_hbm, items.at[0]), (ratings_hbm.at[0], ratings), (unoise_hbm, unoise), (inoise_hbm, inoise))
    loads = [pltpu.make_async_copy(a, b, load.at[i]) for i, (a, b) in enumerate(pairs)]
    for cp in loads[:4]:
        cp.start()

    barrier = pltpu.get_barrier_semaphore()

    def hello(dev):
        pl.semaphore_signal(barrier, inc=1, device_id=dev, device_id_type=MESH)

    def hello_plane(i, _):
        xx, yy = plane_peer(i)
        hello((z, xx, yy, c))
        hello((z, xx, yy, 1 - c))
        return 0

    def hello_z(i, _):
        hello((lax.rem(z + i, NZ), x, y, c))
        return 0

    reach = NZ // 4
    far_z = 2 * reach < NZ - 1
    for dz in range(reach, 0, -1):
        hello_z(dz, 0)
        hello_z(NZ - dz, 0)
    n_hello = 2 * (NP - 1) + 2 * reach + 3
    lax.fori_loop(1, NP, hello_plane, 0)
    hello(partner)
    hello(nxt)
    hello(prv)
    for cp in loads[4:]:
        cp.start()

    def tile_pass(s):
        ub = jnp.concatenate([users[s, 0].astype(BF16), users[s, 1].astype(BF16)], axis=1)
        hb = items[s].astype(BF16)
        count = count_ref[0, s]
        sse = jnp.zeros((1, tile), F32)
        for r in range(grid):
            pred = nt(ub[r * tile:(r + 1) * tile], hb)
            parts = []
            for col in range(grid):
                k = r * grid + col
                slot = jnp.int32(0)
                live = jnp.float32(0.0)
                for t in range(slots):
                    hit = index_ref[s, 0, t] == k
                    slot = jnp.where(hit, jnp.int32(t), slot)
                    live = jnp.where(jnp.logical_and(hit, t < count), jnp.float32(1.0), live)
                e = live * (ratings[s, slot].astype(F32) - pred[:, col * tile:(col + 1) * tile])
                sse = sse + jnp.sum(e * e, axis=0, keepdims=True)
                parts.append(e.astype(BF16))
            row = jnp.concatenate(parts, axis=1)
            err_b[r * tile:(r + 1) * tile, :] = row
            grad_u[r * tile:(r + 1) * tile, :] = jnp.dot(row, hb, preferred_element_type=F32)
        grad_v[...] = tn(err_b[...], ub)
        pay[s, 0:1, :] = sse
        pay[s, 1:2, :] = jnp.broadcast_to(count.astype(F32) * float(tile * tile) / float(tile), (1, tile))

    def sse_z_send(s):
        def body(i, _):
            remote(pay.at[s], sse_z.at[s, z], sz_s.at[s], sz_r.at[s], (lax.rem(z + i, NZ), x, y, c)).start()
            return 0

        lax.fori_loop(1, NZ, body, 0)
        sse_z[s, z] = pay[s]

    def sse_plane_send(s):
        bytes_wait(sse_z.at[s, pl.ds(0, NZ - 1)], sz_r.at[s])
        tot = jnp.sum(sse_z[s], axis=0)
        pay2[s] = tot
        slot = p * 2 + c
        dst = sse_plane.at[s, slot]
        sse_plane[s, slot] = tot
        for xx, yy, d, yyh in peers:
            for cc in (c, 1 - c):
                remote(pay2.at[s], dst, sp_s.at[s], sp_r.at[s], (z, xx, yy, cc)).start()
        remote(pay2.at[s], dst, sp_s.at[s], sp_r.at[s], partner).start()

    def precision_of(s):
        bytes_wait(sse_plane.at[s, pl.ds(0, 2 * NP - 1)], sp_r.at[s])
        tot = jnp.sum(sse_plane[s], axis=0)
        sums = jnp.sum(tot, axis=1, keepdims=True)
        return (1.0 + sums[1:2, :] / 2.0) / (1.0 + sums[0:1, :] / 2.0)

    def update_items(s, precision):
        h = items[s]
        dst = new_items.at[s] if s + 1 < strata else items_out
        dst[...] = (h + step_size * (jnp.broadcast_to(precision, (1, rank)) * grad_v[...] - item_prec * h)
                        + noise_scale * inoise[s].astype(F32))

    def shift(s):
        remote(new_items.at[s], items.at[s + 1], sh_s.at[s], sh_r.at[s], nxt).start()

    def update_users(s, precision):
        pr = jnp.broadcast_to(precision, (1, half))
        for h in range(2):
            u = users[s, h]
            cols = slice(h * half, (h + 1) * half)
            new = (u + step_size * (pr * grad_u[:, cols] - prior_prec * (u - mean[s, h]))
                   + noise_scale * unoise[s][:, cols].astype(F32))
            if s + 1 < strata:
                users[s + 1, h] = new
            else:
                users_out[:, cols] = new

    def users_to_partner(s):
        remote(users.at[s, 1 - c], users_in.at[s - 1], ux_s.at[s - 1], ux_r.at[s - 1], partner).start()

    odd = lax.rem(z, 2)

    def pair(j):
        up = T2 // 2 + j * (1 - 2 * odd)
        down = T2 // 2 - 1 - j + odd * (2 + 2 * j)
        return lax.rem(z // 2 + up, T2), lax.rem(z // 2 + down, T2)

    groups = [t for j in range(pairs_z) for t in pair(j)]

    def group(ref, t):
        return ref[pl.ds(pl.multiple_of(t * span, 128), span), :]

    def group_send(k, i, t):
        for xx, yy, d, yyh in peers:
            remote(g_sum.at[k, t, pars[d], xx, yyh], plane_in.at[k, i, p], prs_s.at[k], prs_r.at[k, i], (z, xx, yy, c)).start()
        plane_in[k, i, p] = g_sum[k, t, par, x, yh]

    def plane_sum_z_send(k, some):
        for i in some:
            t = groups[i]
            bytes_wait(plane_in.at[k, i, pl.ds(0, NP - 1)], prs_r.at[k, i])
            acc = plane_in[k, i, 0]
            for q in range(1, NP):
                acc = acc + plane_in[k, i, q]
            z_out[k, i] = acc

            def send():
                remote(z_out.at[k, i], z_in.at[k, z], zrs_s.at[k], zrs_r.at[k], (2 * t + par, x, y, c)).start()

            if i == T2 - 1:
                pl.when(other)(send)
            else:
                send()

    def z_sum(k):
        z_in[k, z] = z_out[k, T2 - 1]
        bytes_wait(z_in.at[k, pl.ds(0, NZ - 1)], zrs_r.at[k])
        g = z_in[k, 0]
        for n in range(1, NZ):
            g = g + z_in[k, n]
        return g

    def step_weights(g):
        w = w_own[...]
        w = w + rate * (prior_prec * g - weight_decay * w)
        w_own[...] = w
        return w

    def weights_along_z(s):
        @pl.when(owner)
        def _():
            wz[s, z // 2] = step_weights(z_sum(s))

            def body(i, _):
                for d in (T2 - i, T2 + i):
                    remote(wz.at[s, z // 2], wz.at[s, z // 2], zag_s.at[s], zag_r.at[s, z // 2],
                           (lax.rem(z + d, NZ), x, y, c)).start()
                return 0

            remote(wz.at[s, z // 2], wz.at[s, z // 2], zag_s.at[s], zag_r.at[s, z // 2],
                   (lax.rem(z + T2, NZ), x, y, c)).start()
            lax.fori_loop(1, T2, body, 0)

    def weights_over_plane(s, some):
        for i in some:
            t = groups[i]

            def arrived():
                bytes_wait(wz.at[s, t], zag_r.at[s, t])

            if i == T2 - 1:
                pl.when(other)(arrived)
            else:
                arrived()
            for xx, yy, d, yyh in peers:
                remote(wz.at[s, t], wfull.at[s, t, par, x, yh], pag_s.at[s], pag_r.at[s, i // 2], (z, xx, yy, c)).start()
            wfull[s, t, par, x, yh] = wz[s, t]

    def mean_of_both(s):
        acc = None
        for j in range(pairs_z - 1, -1, -1):
            bytes_wait(share.at[pl.ds(0, 2)], pag_r.at[s, j])
            t0, t1 = pair(j)
            w = jnp.concatenate([wfull[s, t].reshape(span, half).astype(BF16) for t in (t0, t1)], axis=0)
            f = jnp.concatenate([feat[:, pl.ds(pl.multiple_of(t * span, 128), span)] for t in (t0, t1)], axis=1)
            part = jnp.dot(f, w, preferred_element_type=F32)
            acc = part if acc is None else acc + part
        return acc

    def means_to_partner(s, m):
        mean_send[s - 1] = m[rows:]
        remote(mean_send.at[s - 1], mean.at[s, c], mx_s.at[s - 1], mx_r.at[s - 1], partner).start()

    loads[0].wait()
    loads[1].wait()
    wb[...] = w0[...].astype(BF16)
    for i in range(rows // 128):
        featT[:, i * 128:(i + 1) * 128] = feat[i * 128:(i + 1) * 128, :].T
    t_own = z * (NP // 2) + p // 2
    own8 = w0[pl.ds(pl.multiple_of(t_own * R8, 8), R8), :]
    w_own[...] = jnp.where(c == 0, own8[:, :half], own8[:, half:])
    m = jnp.dot(feat[0:rows], wb[...], preferred_element_type=F32)
    loads[2].wait()
    loads[3].wait()
    for h in range(2):
        mh = m[:, h * half:(h + 1) * half]
        mean[0, h] = mh
        off[h] = (users[0, h] - mh).astype(BF16)
    shape = ce_send.shape[1:]
    lag = 3
    for n in range(T2 + lag):
        if n < T2:
            t = groups[n]
            ce_send[t] = jnp.dot(group(featT, t)[:, 0:rows], off[1 - c], preferred_element_type=F32).reshape(shape)
            if n == 0:
                pl.semaphore_wait(barrier, n_hello)
                if far_z:
                    for dz in (reach, NZ - reach):
                        pl.semaphore_signal(met, inc=1, device_id=(lax.rem(z + dz, NZ), x, y, c), device_id_type=MESH)
            remote(ce_send.at[t], ce_in.at[t], ce_s, ce_r.at[n], partner).start()
        if n >= lag:
            i, t = n - lag, groups[n - lag]
            g = jnp.dot(group(featT, t)[:, 0:rows], off[c], preferred_element_type=F32).reshape(shape)
            bytes_wait(ce_in.at[t], ce_r.at[i])
            g_sum[0, t] = g + ce_in[t]
            group_send(0, i, t)
    loads[4].wait()
    loads[5].wait()
    tile_pass(0)
    if far_z:
        pl.semaphore_wait(met, 2)
    sse_z_send(0)
    feat_out[...] = feat[0:rows].astype(F32)
    remote(feat_out, feat_in, fx_s, fx_r, partner).start()
    plane_sum_z_send(0, range(T2))
    sse_plane_send(0)
    bytes_wait(feat_in, fx_r)
    feat[rows:, :] = feat_in[...].astype(BF16)
    for i in range(rows // 128):
        featT[:, rows + i * 128:rows + (i + 1) * 128] = feat[rows + i * 128:rows + (i + 1) * 128, :].T
    for cp in loads[6:]:
        cp.wait()
    for s in range(strata - 1):
        weights_along_z(s)
        weights_over_plane(s, range(T2 - 1, T2 // 2 - 2, -1))
        precision = precision_of(s)
        if s > 0:
            bytes_wait(mean.at[s, 0], mx_r.at[s - 1])
        update_users(s, precision)
        users_to_partner(s + 1)
        update_items(s, precision)
        weights_over_plane(s, range(T2 // 2 - 2, -1, -1))
        shift(s)
        n = s + 1
        m = mean_of_both(s)
        bytes_wait(users_in.at[s], ux_r.at[s])
        o = jnp.concatenate([users[n, c] - m[:rows], users_in[s] - m[rows:]], axis=0).astype(BF16)

        def send_groups(some):
            for i in some:
                t = groups[i]
                g_sum[n, t] = jnp.dot(group(featT, t), o, preferred_element_type=F32).reshape(shape)
                group_send(n, i, t)

        first = T2 // 2 if n + 1 < strata else T2 // 4
        send_groups(range(first))
        bytes_wait(items.at[n], sh_r.at[s])
        tile_pass(n)
        sse_z_send(n)
        send_groups(range(first, T2))
        mean[n, c] = m[:rows]
        means_to_partner(n, m)
        cut = T2 if n + 1 < strata else T2 // 2 + 1
        plane_sum_z_send(n, range(cut))
        sse_plane_send(n)
        plane_sum_z_send(n, range(cut, T2))

    @pl.when(owner)
    def _():
        w = step_weights(z_sum(strata - 1))
        fin[c] = w
        for n, dev in enumerate((partner, (z, x, y + 1 - 2 * par, c), (z, x, y + 1 - 2 * par, 1 - c))):
            remote(w_own, fin.at[c], fin_s.at[n], fin_r.at[c], dev).start()

    e = strata - 1
    bytes_wait(mean.at[e, 0], mx_r.at[e - 1])
    precision = precision_of(e)
    update_items(e, precision)
    update_users(e, precision)

    @pl.when(owner)
    def _():
        bytes_wait(fin.at[0], fin_r.at[1 - c])

    @pl.when(other)
    def _():
        bytes_wait(fin.at[0], fin_r.at[0])
        bytes_wait(fin.at[1], fin_r.at[1])

    r2 = R8 // 4
    for h in range(2):
        t8 = fin[h]
        o2 = t8[0:r2]
        for k in range(1, 4):
            o2 = jnp.where(par * 2 + c == k, t8[r2 * k:r2 * (k + 1)], o2)
        weights_out[:, h * half:(h + 1) * half] = o2

    bytes_wait(ce_send, ce_s)
    bytes_wait(feat_out, fx_s)
    for s in range(strata - 1):
        bytes_wait(users_in.at[s], ux_s.at[s])
        bytes_wait(mean_send.at[s], mx_s.at[s])
        bytes_wait(new_items.at[s], sh_s.at[s])
        bytes_wait(share, pag_s.at[s])
    for k in range(jobs):
        bytes_wait(share, prs_s.at[k])

    @pl.when(owner)
    def _():
        for k in range(jobs):
            bytes_wait(z_out.at[k, pl.ds(0, T2 - 1)], zrs_s.at[k])
        for s in range(strata - 1):
            bytes_wait(z_in.at[s, pl.ds(0, NZ - 1)], zag_s.at[s])
        for n in range(3):
            bytes_wait(w_own, fin_s.at[n])

    @pl.when(other)
    def _():
        for k in range(jobs):
            bytes_wait(z_out.at[k], zrs_s.at[k])

    for s in range(strata):
        bytes_wait(sse_plane.at[s, pl.ds(0, 2 * NP - 1)], sp_s.at[s])
        bytes_wait(sse_z.at[s, pl.ds(0, NZ - 1)], sz_s.at[s])


def in_place(array):
    return pltpu.with_memory_space_constraint(array, pltpu.HBM)


def local(ratings, tile_index, tile_count, side, users, items, weights, unoise, inoise):
    nz, nx, ny = (lax.axis_size(a) for a in USER[:3])
    strata, slots, tile = ratings.shape[1:4]
    rows, rank = users.shape
    featn = side.shape[1]
    npl, t2, half = nx * ny, nz // 2, rank // 2
    r8 = featn // (t2 * npl)
    jobs = 3
    dims = (nz, nx, ny, strata, slots, tile, rows, featn, rank)
    g_shape = (t2, 2, nx, ny // 2, r8, half)
    V, D = pltpu.VMEM, pltpu.SemaphoreType.DMA
    data = [
        V((strata, slots, tile, tile), BF16),
        V((2 * rows, featn), BF16),
        V((featn, 2 * rows), BF16),
        V((rows, featn), F32),
        V((rows, featn), F32),
        V((strata, 2, rows, half), F32),
        V((strata - 1, rows, half), F32),
        V((strata, rows, rank), F32),
        V((strata - 1, rows, rank), F32),
        V((featn, rank), F32),
        V((featn, rank), BF16),
        V((strata, rows, rank), BF16),
        V((strata, rows, rank), BF16),
        V((strata, 2, rows, half), F32),
        V((strata - 1, rows, half), F32),
        V((2, rows, half), BF16),
        V((rows, rows), BF16),
        V((rows, rank), F32),
        V((rows, rank), F32),
        V(g_shape, F32),
        V(g_shape, F32),
        V((jobs, *g_shape), F32),
        V((jobs, t2, npl, r8, half), F32),
        V((jobs, t2, r8, half), F32),
        V((jobs, nz, r8, half), F32),
        V((r8, half), F32),
        V((strata - 1, t2, r8, half), F32),
        V((strata - 1, *g_shape), F32),
        V((strata, 2, tile), F32),
        V((strata, 2 * npl, 2, tile), F32),
        V((strata, 2, tile), F32),
        V((strata, nz, 2, tile), F32),
        V((2, r8, half), F32),
    ]
    sems = [
        D((8,)),
        D(()), D((t2,)),
        D(()), D(()),
        D((strata - 1,)), D((strata - 1,)),
        D((strata - 1,)), D((strata - 1,)),
        D((jobs,)), D((jobs, t2)),
        D((jobs,)), D((jobs,)),
        D((strata - 1,)), D((strata - 1, t2)),
        D((strata - 1,)), D((strata - 1, t2 // 2)),
        D((strata,)), D((strata,)),
        D((strata,)), D((strata,)),
        D((strata - 1,)), D((strata - 1,)),
        D((3,)), D((2,)),
        pltpu.SemaphoreType.REGULAR,
    ]
    any_ = pl.BlockSpec(memory_space=pltpu.HBM)
    vmem = pl.BlockSpec(memory_space=pltpu.VMEM)
    smem = pl.BlockSpec(memory_space=pltpu.SMEM)
    return pl.pallas_call(
        functools.partial(kernel, dims),
        out_shape=(
            jax.ShapeDtypeStruct((rows, rank), F32),
            jax.ShapeDtypeStruct((rows, rank), F32),
            jax.ShapeDtypeStruct((r8 // 4, rank), F32),
        ),
        in_specs=[smem, smem] + [any_] * 7,
        out_specs=(vmem, vmem, vmem),
        scratch_shapes=data + sems,
        compiler_params=pltpu.CompilerParams(collective_id=0, has_side_effects=True, vmem_limit_bytes=53 * 1024 * 1024),
        name="sweep",
    )(in_place(jnp.transpose(tile_index, (1, 0, 2))), in_place(tile_count), ratings, side, users, items, weights, unoise, inoise)


def finer_of(mesh):
    return Mesh(mesh.devices.reshape(16, 4, 4, 2), USER)


def solution(mesh):
    return over(finer_of(mesh))


def over(finer):
    return jax.shard_map(
        local,
        mesh=finer,
        in_specs=(
            P(USER, None, None, None, None),
            P(USER, None, None),
            P(USER, None),
            P(USER, None),
            P(USER, None),
            P(USER, None),
            P(),
            P(None, USER, None),
            P(None, USER, None),
        ),
        out_specs=(P(USER, None), P(USER, None), P(USER, None)),
        check_vma=False,
    )
```
